32 devices in a mesh: section: 2 (over y), seq: 16 (over z, x, core).
Axes of the slice: x: 2, y: 2, z: 4, core: 2. Of those that a mesh axis runs over, the one named last changes fastest.
Arguments:
- queries: bfloat16 [2, 2048, 1024], P('section', 'seq'), may hold values from -35 to 35
- keys: bfloat16 [2, 2048, 1024], P('section', 'seq'), may hold values from -4 to 4
- values: bfloat16 [2, 2048, 1024], P('section', 'seq'), may hold values from -6 to 6
- upstream: bfloat16 [2, 2048, 1024], P('section', 'seq'), may hold values from -6 to 6
- neighbours: int32 [16, 6], replicated, may hold values from 0 to 15, as said below
- counts: int32 [16], replicated, may hold values from 1 to 6, as said below
Outputs:
- query_grad: bfloat16 [2, 2048, 1024], P('section', 'seq')
- key_grad: bfloat16 [2, 2048, 1024], P('section', 'seq')
- value_grad: bfloat16 [2, 2048, 1024], P('section', 'seq')
The draws below stay inside these ranges and needn't reach their ends.
Inputs may be any that keep to these rules, and one draw needn't show every extreme that they name: Row a lists 6 different tiles, the first being a itself; only the first counts[a] of them are neighbours of a. `counts`: some tile has 6 neighbour tiles and some tile has only itself.
All inputs are finite; a program needn't handle non-finite values.
Results may differ from the reference program's by a relative error of at most 0.009.
Values may be sent and summed in bfloat16 or wider, within the bound.
A program may use at most 64 MiB of HBM per device.

```python
import jax
import jax.numpy as jnp
from jax import lax

HEADS = 16
DH = 64
D = 1024
TILE = 128
MAXNB = 6
LAYERS = 2
TILES = 16
ATOMS = 2048


def paired_draw(key):
    key_query, key_key = jax.random.split(jax.random.fold_in(key, 11), 2)
    shape = (LAYERS, ATOMS, D)
    query_part = jnp.clip(jax.random.normal(key_query, shape, jnp.float32), -4.0, 4.0)
    key_part = jnp.clip(jax.random.normal(key_key, shape, jnp.float32), -4.0, 4.0)
    return (query_part, key_part)


def draw_queries(key, part):
    return paired_draw(key)[0].astype(jnp.bfloat16)


def draw_keys(key, part):
    return paired_draw(key)[1].astype(jnp.bfloat16)


def draw_neighbours(key, part):
    raw = jax.random.randint(jax.random.fold_in(key, 3), (TILES, TILES), 0, 2 ** 20)
    ranked = raw * TILES + lax.broadcasted_iota(jnp.int32, (TILES, TILES), 1)
    diagonal = lax.broadcasted_iota(jnp.int32, (TILES, TILES), 0) == lax.broadcasted_iota(jnp.int32, (TILES, TILES), 1)
    ranked = jnp.where(diagonal, -1, ranked)
    order = jnp.argsort(ranked, axis=1, stable=True)
    return order[:, :MAXNB].astype(jnp.int32)


def draw_counts(key, part):
    key_base, key_first, key_second = jax.random.split(jax.random.fold_in(key, 5), 3)
    drawn = jax.random.randint(key_base, (TILES,), 1, MAXNB + 1)
    first_pos = jax.random.randint(key_first, (), 0, TILES)
    second_pos = (first_pos + jax.random.randint(key_second, (), 1, TILES)) % TILES
    drawn = drawn.at[first_pos].set(MAXNB).at[second_pos].set(1)
    return drawn.astype(jnp.int32)


def block_scale(own_key, shape, pieces, low, high):
    loudness, own = 1.0, jax.random.fold_in(own_key, 6)
    for axis_at, shards_of in pieces:
        draws = jnp.exp(jax.random.uniform(jax.random.fold_in(own, axis_at), (shards_of,), jnp.float32, low / len(pieces), high / len(pieces)))
        loudness = loudness * jnp.repeat(draws, shape[axis_at] // shards_of).reshape([-1 if axis == axis_at else 1 for axis in range(len(shape))])
    return loudness


def normal_values(stream_key, dims, spread, bound, cuts=(), held_as=jnp.bfloat16):
    values = spread * jax.random.normal(stream_key, dims, jnp.float32)
    if cuts:
        values = values * block_scale(stream_key, dims, cuts, -0.22, 0.18)
    return jnp.clip(values, -bound, bound).astype(held_as)


def setup_inputs(seed: int = 0) -> dict:
    key_of = jax.random.split(jax.random.key(seed), 7)
    queries = draw_queries(jax.random.fold_in(key_of[6], 71), 0)
    keys = draw_keys(jax.random.fold_in(key_of[6], 71), 0)
    values = normal_values(key_of[2], (LAYERS, ATOMS, D), 1.0, 6.0, ((0, 2), (1, 16)))
    upstream = normal_values(key_of[3], (LAYERS, ATOMS, D), 1.0, 6.0, ((0, 2), (1, 16)))
    neighbours = draw_neighbours(jax.random.fold_in(key_of[6], 71), 0)
    counts = draw_counts(jax.random.fold_in(key_of[6], 71), 0)
    return dict(queries=queries, keys=keys, values=values, upstream=upstream, neighbours=neighbours, counts=counts)


MASKED = -1e30


def tile_grads(query_t, key_t, value_t, adjoint_t, neighbours, valid):
    score_scale = DH ** -0.5
    key_blk = key_t[neighbours]
    value_blk = value_t[neighbours]
    alive_slots = valid[:, :, None, None]
    scores = jnp.einsum("aie,asje->asij", query_t, key_blk) * score_scale
    scores = jnp.where(alive_slots > 0, scores, MASKED)
    row_peak = jnp.max(scores, axis=(1, 3), keepdims=True)
    weights = jnp.exp(scores - row_peak) * alive_slots
    prob_full = weights / jnp.sum(weights, axis=(1, 3), keepdims=True)
    probs_low = prob_full.astype(jnp.bfloat16).astype(jnp.float32)
    dprobs = jnp.einsum("aie,asje->asij", adjoint_t, value_blk)
    delta_sum = jnp.sum(prob_full * dprobs, axis=(1, 3), keepdims=True)
    dscores = (prob_full * (dprobs - delta_sum) * score_scale).astype(jnp.bfloat16).astype(jnp.float32)
    query_out = jnp.einsum("asij,asje->aie", dscores, key_blk)
    key_terms = jnp.einsum("asij,aie->asje", dscores, query_t)
    value_terms = jnp.einsum("asij,aie->asje", probs_low, adjoint_t)
    flat_ids = neighbours.reshape(-1)
    key_out = jnp.zeros((TILES, TILE, DH), jnp.float32).at[flat_ids].add(key_terms.reshape(-1, TILE, DH))
    value_out = jnp.zeros((TILES, TILE, DH), jnp.float32).at[flat_ids].add(value_terms.reshape(-1, TILE, DH))
    return query_out, key_out, value_out


def split_heads(block):
    return block.astype(jnp.float32).reshape(TILES, TILE, HEADS, DH).transpose(2, 0, 1, 3)


def merge_heads(block):
    return block.transpose(1, 2, 0, 3).reshape(ATOMS, HEADS * DH).astype(jnp.bfloat16)


def reference(queries, keys, values, upstream, neighbours, counts):
    adjoints = jnp.roll(upstream, -1, axis=0)
    valid = (jnp.arange(MAXNB, dtype=jnp.int32)[None, :] < counts[:, None]).astype(jnp.float32)

    def per_layer(layer_in):
        split_in = tuple(split_heads(block) for block in layer_in)

        def per_head(head_in):
            return tile_grads(head_in[0], head_in[1], head_in[2], head_in[3], neighbours, valid)

        query_out, key_out, value_out = lax.map(per_head, split_in)
        return merge_heads(query_out), merge_heads(key_out), merge_heads(value_out)

    query_grad, key_grad, value_grad = lax.map(per_layer, (queries, keys, values, adjoints))
    return query_grad, key_grad, value_grad
```

```python
import functools
import math

import jax
import jax.numpy as jnp
from jax import lax
from jax.experimental import pallas as pl
from jax.experimental.pallas import tpu as pltpu
from jax.sharding import PartitionSpec as P

HEADS = 16
DH = 64
TILE = 128
MAXNB = 6
MASKED = -1e30
MESH = pl.DeviceIdType.MESH
EXPONENT = DH ** (-0.5) * math.log2(math.e)
NT = (((1,), (1,)), ((), ()))


def kernel(
    sections,
    tiles,
    near_ref,
    count_ref,
    q_ref,
    k_ref,
    v_ref,
    u_ref,
    dq_ref,
    dk_ref,
    dv_ref,
    q_send,
    k_send,
    v_send,
    u_send,
    q_got,
    k_got,
    v_got,
    u_got,
    k_rows,
    v_rows,
    ds_all,
    pr_all,
    dq_send,
    dk_send,
    dv_send,
    dq_got,
    dk_got,
    dv_got,
    slot_ref,
    send_sem,
    recv_sem,
    q_sem,
    u_sem,
):
    section = lax.axis_index("section")
    me = lax.axis_index("seq")
    group = me // HEADS
    head = me % HEADS
    behind = lax.rem(section + sections - 1, sections)
    ahead = lax.rem(section + 1, sections)
    pairs = HEADS * MAXNB

    barrier = pltpu.get_barrier_semaphore()

    def greet(r, c):
        pl.semaphore_signal(
            barrier, inc=1, device_id=(section, lax.rem(me + r, tiles)), device_id_type=MESH
        )
        return c

    def greet_ahead(h, c):
        pl.semaphore_signal(
            barrier, inc=1, device_id=(ahead, group * HEADS + h), device_id_type=MESH
        )
        return c

    lax.fori_loop(1, tiles, greet, 0)
    lax.fori_loop(0, HEADS, greet_ahead, 0)

    def turn(src, dst):
        for c in range(HEADS // 2):
            flipped = src[:, c * 128 : (c + 1) * 128].T
            dst[2 * c] = flipped[:DH]
            dst[2 * c + 1] = flipped[DH:]

    turn(k_ref, k_send)
    turn(v_ref, v_send)
    turn(q_ref, q_send)
    turn(u_ref, u_send)
    pl.semaphore_wait(barrier, tiles - 1 + HEADS)

    def remote(src, dst, sent, got, where, peer):
        return pltpu.make_async_remote_copy(
            src_ref=src,
            dst_ref=dst,
            send_sem=sent,
            recv_sem=got,
            device_id=(where, peer),
            device_id_type=MESH,
        )

    def send_kv(r, c):
        peer = lax.rem(me + r, tiles)
        block = peer % HEADS
        remote(
            k_send.at[block], k_got.at[me], send_sem.at[0], recv_sem.at[0], section, peer
        ).start()
        remote(
            v_send.at[block], v_got.at[me], send_sem.at[1], recv_sem.at[1], section, peer
        ).start()
        return c

    lax.fori_loop(1, tiles, send_kv, 0)

    def send_qu(r, c):
        h = lax.rem(head + r, HEADS)
        peer = group * HEADS + h
        remote(
            q_send.at[h], q_got.at[head], send_sem.at[2], q_sem.at[head], section, peer
        ).start()
        remote(
            u_send.at[h], u_got.at[head], send_sem.at[3], u_sem.at[head], behind, peer
        ).start()
        return c

    remote(
        u_send.at[head], u_got.at[head], send_sem.at[3], u_sem.at[head], behind, me
    ).start()
    lax.fori_loop(1, HEADS, send_qu, 0)

    k_got[me] = k_send[head]
    v_got[me] = v_send[head]
    q_got[head] = q_send[head]
    ds_all[pairs] = jnp.zeros((TILE, TILE), jnp.bfloat16)
    pr_all[pairs] = jnp.zeros((TILE, TILE), jnp.bfloat16)

    def find(a, c):
        tile = group * HEADS + a
        live = count_ref[tile]
        listed = [
            jnp.where(s < live, near_ref[tile, s], -1) for s in range(MAXNB)
        ]

        def one(b, c):
            found = jnp.int32(pairs)
            for s in range(MAXNB):
                found = jnp.where(listed[s] == b, a * MAXNB + s, found)
            slot_ref[b, a] = found
            return c

        return lax.fori_loop(0, tiles, one, c)

    lax.fori_loop(0, HEADS, find, 0)

    def settle(buffer, count, semaphore):
        part = buffer.at[pl.ds(0, count)]
        pltpu.make_async_copy(part, part, semaphore).wait()

    settle(k_got, tiles - 1, recv_sem.at[0])
    settle(v_got, tiles - 1, recv_sem.at[1])

    def upright(b, c):
        k_rows[b] = k_got[b].T
        v_rows[b] = v_got[b].T
        return c

    lax.fori_loop(0, tiles, upright, 0)

    def query_tile(a):
        tile = group * HEADS + a
        live = count_ref[tile]
        query = q_got[a]
        adjoint = u_got[a]
        near = [near_ref[tile, s] for s in range(MAXNB)]
        scores = []
        for s in range(MAXNB):
            raw = jnp.dot(k_rows[near[s]], query, preferred_element_type=jnp.float32)
            scores.append(jnp.where(s < live, raw, MASKED) if s else raw)
        peak = functools.reduce(
            jnp.maximum, [jnp.max(raw, axis=0, keepdims=True) for raw in scores]
        )
        weights = [jnp.exp2((raw - peak) * EXPONENT) for raw in scores]
        total = sum(jnp.sum(w, axis=0, keepdims=True) for w in weights)
        share = 1.0 / total
        dprobs = [
            jnp.dot(v_rows[near[s]], adjoint, preferred_element_type=jnp.float32)
            for s in range(MAXNB)
        ]
        delta = share * sum(
            jnp.sum(w * d, axis=0, keepdims=True) for w, d in zip(weights, dprobs)
        )
        scaled = share * (DH ** (-0.5))
        out = jnp.zeros((DH, TILE), jnp.float32)
        for s in range(MAXNB):
            pr_all[a * MAXNB + s] = (weights[s] * share).astype(jnp.bfloat16)
            dscore = ((weights[s] * scaled) * (dprobs[s] - delta)).astype(jnp.bfloat16)
            ds_all[a * MAXNB + s] = dscore
            out += jnp.dot(k_got[near[s]], dscore, preferred_element_type=jnp.float32)
        dq_send[a] = out.astype(jnp.bfloat16)

    def await_u(a):
        pltpu.make_async_copy(u_got.at[a], u_got.at[a], u_sem.at[a]).wait()

    await_u(head)
    query_tile(head)
    dq_got[head] = dq_send[head]

    def query_step(r, c):
        a = lax.rem(head + HEADS - r, HEADS)
        pltpu.make_async_copy(q_got.at[a], q_got.at[a], q_sem.at[a]).wait()
        await_u(a)
        query_tile(a)
        remote(
            dq_send.at[a],
            dq_got.at[head],
            send_sem.at[4],
            recv_sem.at[2],
            section,
            group * HEADS + a,
        ).start()
        return c

    lax.fori_loop(1, HEADS, query_step, 0)

    def key_tile(b):
        key_sum = jnp.zeros((DH, TILE), jnp.float32)
        value_sum = jnp.zeros((DH, TILE), jnp.float32)
        for a in range(HEADS):
            slot = slot_ref[b, a]
            key_sum += lax.dot_general(
                q_got[a], ds_all[slot], NT, preferred_element_type=jnp.float32
            )
            value_sum += lax.dot_general(
                u_got[a], pr_all[slot], NT, preferred_element_type=jnp.float32
            )
        dk_send[b] = key_sum.astype(jnp.bfloat16)
        dv_send[b] = value_sum.astype(jnp.bfloat16)

    def key_step(r, c):
        b = lax.rem(me + r, tiles)
        key_tile(b)
        remote(
            dk_send.at[b], dk_got.at[me], send_sem.at[5], recv_sem.at[3], section, b
        ).start()
        remote(
            dv_send.at[b], dv_got.at[me], send_sem.at[6], recv_sem.at[4], section, b
        ).start()
        return c

    lax.fori_loop(1, tiles, key_step, 0)
    key_tile(me)
    dk_got[me] = dk_send[me]
    dv_got[me] = dv_send[me]

    def unturn(src, dst):
        for c in range(HEADS // 2):
            parts = []
            for h in (2 * c, 2 * c + 1):
                if tiles == HEADS or src is dq_got:
                    parts.append(src[h])
                else:
                    parts.append(
                        sum(
                            src[g * HEADS + h].astype(jnp.float32)
                            for g in range(tiles // HEADS)
                        ).astype(jnp.bfloat16)
                    )
            dst[:, c * 128 : (c + 1) * 128] = jnp.concatenate(parts, axis=0).T

    settle(dq_got, HEADS - 1, recv_sem.at[2])
    unturn(dq_got, dq_ref)
    settle(dk_got, tiles - 1, recv_sem.at[3])
    unturn(dk_got, dk_ref)
    settle(dv_got, tiles - 1, recv_sem.at[4])
    unturn(dv_got, dv_ref)

    settle(k_got, tiles - 1, send_sem.at[0])
    settle(v_got, tiles - 1, send_sem.at[1])
    settle(q_got, HEADS - 1, send_sem.at[2])
    settle(u_got, HEADS, send_sem.at[3])
    settle(dq_got, HEADS - 1, send_sem.at[4])
    settle(dk_got, tiles - 1, send_sem.at[5])
    settle(dv_got, tiles - 1, send_sem.at[6])


def per_device(queries, keys, values, upstream, neighbours, counts):
    sections = lax.axis_size("section")
    tiles = lax.axis_size("seq")
    rows, width = queries.shape[1:]
    assert rows == TILE and width == HEADS * DH and tiles % HEADS == 0
    vmem = pl.BlockSpec(memory_space=pltpu.VMEM)
    smem = pl.BlockSpec(memory_space=pltpu.SMEM)
    out = jax.ShapeDtypeStruct((rows, width), jnp.bfloat16)

    def blocks(count):
        return pltpu.VMEM((count, DH, TILE), jnp.bfloat16)

    pairs = HEADS * MAXNB + 1
    dq, dk, dv = pl.pallas_call(
        functools.partial(kernel, sections, tiles),
        out_shape=(out, out, out),
        in_specs=[smem, smem, vmem, vmem, vmem, vmem],
        out_specs=(vmem, vmem, vmem),
        scratch_shapes=[blocks(HEADS)] * 4
        + [blocks(HEADS), blocks(tiles), blocks(tiles), blocks(HEADS)]
        + [pltpu.VMEM((tiles, TILE, DH), jnp.bfloat16)] * 2
        + [pltpu.VMEM((pairs, TILE, TILE), jnp.bfloat16)] * 2
        + [blocks(HEADS), blocks(tiles), blocks(tiles)]
        + [blocks(HEADS), blocks(tiles), blocks(tiles)]
        + [
            pltpu.SMEM((tiles, HEADS), jnp.int32),
            pltpu.SemaphoreType.DMA((7,)),
            pltpu.SemaphoreType.DMA((5,)),
            pltpu.SemaphoreType.DMA((HEADS,)),
            pltpu.SemaphoreType.DMA((HEADS,)),
        ],
        compiler_params=pltpu.CompilerParams(
            collective_id=0, has_side_effects=True, vmem_limit_bytes=60 * 1024 * 1024
        ),
    )(neighbours, counts, queries[0], keys[0], values[0], upstream[0])
    return dq[None], dk[None], dv[None]


def solution(mesh):
    spec = P("section", "seq", None)
    return jax.shard_map(
        per_device,
        mesh=mesh,
        in_specs=(spec, spec, spec, spec, P(), P()),
        out_specs=(spec, spec, spec),
        check_vma=False,
    )
```

```python
import functools
import math

import jax
import jax.numpy as jnp
from jax import lax
from jax.experimental import pallas as pl
from jax.experimental.pallas import tpu as pltpu
from jax.sharding import PartitionSpec as P

HEADS = 16
DH = 64
TILE = 128
MAXNB = 6
MASKED = -1e30
MESH = pl.DeviceIdType.MESH
EXPONENT = DH ** (-0.5) * math.log2(math.e)
NT = (((1,), (1,)), ((), ()))


def sweep(step, n):
    lax.fori_loop(1, n, step, 0)


def kernel(
    sections,
    tiles,
    near_ref,
    count_ref,
    q_ref,
    k_ref,
    v_ref,
    u_ref,
    dq_got,
    dk_got,
    dv_got,
    q_in,
    k_in,
    v_in,
    u_in,
    q_send,
    k_send,
    v_send,
    u_send,
    q_got,
    k_got,
    v_got,
    u_got,
    k_rows,
    v_rows,
    ds_all,
    pr_all,
    dq_send,
    dk_send,
    dv_send,
    p_all,
    slot_ref,
    load_sem,
    send_sem,
    recv_sem,
    q_sem,
    u_sem,
):
    section = lax.axis_index("section")
    me = lax.axis_index("seq")
    group = me // HEADS
    head = me % HEADS
    behind = lax.rem(section + sections - 1, sections)
    ahead = lax.rem(section + 1, sections)
    pairs = HEADS * MAXNB

    loads = [
        pltpu.make_async_copy(src, dst, load_sem.at[i])
        for i, (src, dst) in enumerate(
            ((k_ref, k_in), (q_ref, q_in), (v_ref, v_in), (u_ref, u_in))
        )
    ]
    for load in loads:
        load.start()
    barrier = pltpu.get_barrier_semaphore()

    def greet(r, c):
        pl.semaphore_signal(
            barrier, inc=1, device_id=(section, lax.rem(me + r, tiles)), device_id_type=MESH
        )
        return c

    def greet_ahead(h, c):
        pl.semaphore_signal(
            barrier, inc=1, device_id=(ahead, group * HEADS + h), device_id_type=MESH
        )
        return c

    lax.fori_loop(1, tiles, greet, 0)
    lax.fori_loop(0, HEADS, greet_ahead, 0)

    def turn(src, dst):
        for c in range(HEADS // 2):
            flipped = src[:, c * 128 : (c + 1) * 128].T
            dst[2 * c] = flipped[:DH]
            dst[2 * c + 1] = flipped[DH:]

    loads[0].wait()
    turn(k_in, k_send)
    loads[1].wait()
    turn(q_in, q_send)
    pl.semaphore_wait(barrier, tiles - 1 + HEADS)

    def remote(src, dst, sent, got, where, peer):
        return pltpu.make_async_remote_copy(
            src_ref=src,
            dst_ref=dst,
            send_sem=sent,
            recv_sem=got,
            device_id=(where, peer),
            device_id_type=MESH,
        )

    def send_keys(buffer, landing, index):
        def step(r, c):
            peer = lax.rem(me + r, tiles)
            remote(
                buffer.at[peer % HEADS],
                landing.at[me],
                send_sem.at[index],
                recv_sem.at[index],
                section,
                peer,
            ).start()
            return c

        sweep(step, tiles)

    def send_queries(buffer, landing, index, sem, where, first):
        def step(r, c):
            h = lax.rem(head + r, HEADS)
            remote(
                buffer.at[h],
                landing.at[head],
                send_sem.at[index],
                sem.at[head],
                where,
                group * HEADS + h,
            ).start()
            return c

        if first == 0:
            step(0, 0)
        sweep(step, HEADS)

    send_keys(k_send, k_got, 0)
    send_queries(q_send, q_got, 2, q_sem, section, 1)
    loads[2].wait()
    turn(v_in, v_send)
    send_keys(v_send, v_got, 1)
    loads[3].wait()
    turn(u_in, u_send)
    send_queries(u_send, u_got, 3, u_sem, behind, 0)
    k_got[me] = k_send[head]
    v_got[me] = v_send[head]
    q_got[head] = q_send[head]
    ds_all[pairs] = jnp.zeros((TILE, TILE), jnp.bfloat16)
    pr_all[pairs] = jnp.zeros((TILE, TILE), jnp.bfloat16)

    def find(a, c):
        tile = group * HEADS + a
        live = count_ref[tile]
        listed = [
            jnp.where(s < live, near_ref[s, tile], -1) for s in range(MAXNB)
        ]

        def one(b, c):
            found = jnp.int32(pairs)
            for s in range(MAXNB):
                found = jnp.where(listed[s] == b, a * MAXNB + s, found)
            slot_ref[b, a] = found
            return c

        return lax.fori_loop(0, tiles, one, c)

    lax.fori_loop(0, HEADS, find, 0)

    def settle(buffer, count, semaphore):
        part = buffer.at[pl.ds(0, count)]
        pltpu.make_async_copy(part, part, semaphore).wait()

    def upright(src, dst):
        def step(b, c):
            dst[b] = src[b].T
            return c

        lax.fori_loop(0, tiles, step, 0)

    settle(k_got, tiles - 1, recv_sem.at[0])
    upright(k_got, k_rows)

    def weigh(a):
        tile = group * HEADS + a
        live = count_ref[tile]
        query = q_got[a]
        scores = []
        for s in range(MAXNB):
            raw = jnp.dot(
                k_rows[near_ref[s, tile]], query, preferred_element_type=jnp.float32
            )
            scores.append(jnp.where(s < live, raw, MASKED) if s else raw)
        peak = functools.reduce(
            jnp.maximum, [jnp.max(raw, axis=0, keepdims=True) for raw in scores]
        )
        weights = [jnp.exp2((raw - peak) * EXPONENT) for raw in scores]
        share = 1.0 / sum(jnp.sum(w, axis=0, keepdims=True) for w in weights)
        for s in range(MAXNB):
            prob = weights[s] * share
            p_all[a * MAXNB + s] = prob
            pr_all[a * MAXNB + s] = prob.astype(jnp.bfloat16)

    def weigh_step(r, c):
        a = lax.rem(head + HEADS - r, HEADS)
        pltpu.make_async_copy(q_got.at[a], q_got.at[a], q_sem.at[a]).wait()
        weigh(a)
        return c

    weigh(head)
    lax.fori_loop(1, HEADS, weigh_step, 0)
    settle(v_got, tiles - 1, recv_sem.at[1])
    upright(v_got, v_rows)

    def query_tile(a):
        tile = group * HEADS + a
        pltpu.make_async_copy(u_got.at[a], u_got.at[a], u_sem.at[a]).wait()
        adjoint = u_got[a]
        near = [near_ref[s, tile] for s in range(MAXNB)]
        probs = [p_all[a * MAXNB + s] for s in range(MAXNB)]
        dprobs = [
            jnp.dot(v_rows[near[s]], adjoint, preferred_element_type=jnp.float32)
            for s in range(MAXNB)
        ]
        delta = sum(
            jnp.sum(p * d, axis=0, keepdims=True) for p, d in zip(probs, dprobs)
        )
        out = jnp.zeros((DH, TILE), jnp.float32)
        for s in range(MAXNB):
            dscore = (probs[s] * (dprobs[s] - delta) * (DH ** (-0.5))).astype(jnp.bfloat16)
            ds_all[a * MAXNB + s] = dscore
            out += jnp.dot(k_got[near[s]], dscore, preferred_element_type=jnp.float32)
        dq_send[a] = out.astype(jnp.bfloat16)

    query_tile(head)

    def query_step(r, c):
        a = lax.rem(head + HEADS - r, HEADS)
        query_tile(a)
        remote(
            dq_send.at[a],
            dq_got.at[head],
            send_sem.at[4],
            recv_sem.at[2],
            section,
            group * HEADS + a,
        ).start()
        return c

    lax.fori_loop(1, HEADS, query_step, 0)

    def key_tile(b):
        key_sum = jnp.zeros((DH, TILE), jnp.float32)
        value_sum = jnp.zeros((DH, TILE), jnp.float32)
        for a in range(HEADS):
            slot = slot_ref[b, a]
            key_sum += lax.dot_general(
                q_got[a], ds_all[slot], NT, preferred_element_type=jnp.float32
            )
            value_sum += lax.dot_general(
                u_got[a], pr_all[slot], NT, preferred_element_type=jnp.float32
            )
        dk_send[b] = key_sum.astype(jnp.bfloat16)
        dv_send[b] = value_sum.astype(jnp.bfloat16)

    def key_step(r, c):
        b = lax.rem(me + r, tiles)
        key_tile(b)
        remote(
            dk_send.at[b], dk_got.at[me], send_sem.at[5], recv_sem.at[3], section, b
        ).start()
        remote(
            dv_send.at[b], dv_got.at[me], send_sem.at[6], recv_sem.at[4], section, b
        ).start()
        return c

    sweep(key_step, tiles)
    key_tile(me)
    own = [
        pltpu.make_async_copy(src.at[i], dst.at[i], load_sem.at[n])
        for n, (src, dst, i) in enumerate(
            ((dq_send, dq_got, head), (dk_send, dk_got, me), (dv_send, dv_got, me))
        )
    ]
    for copy in own:
        copy.start()
    for copy in own:
        copy.wait()

    settle(dq_got, HEADS - 1, recv_sem.at[2])
    settle(dk_got, tiles - 1, recv_sem.at[3])
    settle(dv_got, tiles - 1, recv_sem.at[4])
    settle(k_got, tiles - 1, send_sem.at[0])
    settle(v_got, tiles - 1, send_sem.at[1])
    settle(q_got, HEADS - 1, send_sem.at[2])
    settle(u_got, HEADS, send_sem.at[3])
    settle(dq_got, HEADS - 1, send_sem.at[4])
    settle(dk_got, tiles - 1, send_sem.at[5])
    settle(dv_got, tiles - 1, send_sem.at[6])


def unturn(groups, dq_got, dk_got, dv_got, dq_ref, dk_ref, dv_ref, dq, dk, dv, turned, in_sem, out_sem):
    arrays = ((dq_got, dq, dq_ref), (dk_got, dk, dk_ref), (dv_got, dv, dv_ref))
    loads = [
        pltpu.make_async_copy(src, buffer, in_sem.at[n])
        for n, (src, buffer, dst) in enumerate(arrays)
    ]
    for load in loads:
        load.start()
    stores = []
    for n, (src, buffer, dst) in enumerate(arrays):
        loads[n].wait()
        for c in range(HEADS // 2):
            pair = buffer[2 * c : 2 * c + 2]
            if n and groups > 1:
                pair = sum(
                    buffer[g * HEADS + 2 * c : g * HEADS + 2 * c + 2].astype(jnp.float32)
                    for g in range(groups)
                ).astype(jnp.bfloat16)
            turned[n, :, c * 128 : (c + 1) * 128] = pair.reshape(TILE, TILE).T
        stores.append(pltpu.make_async_copy(turned.at[n], dst, out_sem.at[n]))
        stores[n].start()
    for store in stores:
        store.wait()


def per_device(queries, keys, values, upstream, neighbours, counts):
    sections = lax.axis_size("section")
    tiles = lax.axis_size("seq")
    rows, width = queries.shape[1:]
    assert rows == TILE and width == HEADS * DH and tiles % HEADS == 0
    smem = pl.BlockSpec(memory_space=pltpu.SMEM)
    out = jax.ShapeDtypeStruct((rows, width), jnp.bfloat16)

    def blocks(count):
        return pltpu.VMEM((count, DH, TILE), jnp.bfloat16)

    pairs = HEADS * MAXNB + 1
    whole = pl.BlockSpec(memory_space=pl.ANY)

    def shape(count):
        return jax.ShapeDtypeStruct((count, DH, TILE), jnp.bfloat16)

    got = pl.pallas_call(
        functools.partial(kernel, sections, tiles),
        out_shape=(shape(HEADS), shape(tiles), shape(tiles)),
        in_specs=[smem, smem, whole, whole, whole, whole],
        out_specs=(whole,) * 3,
        scratch_shapes=[pltpu.VMEM((rows, width), jnp.bfloat16)] * 4
        + [blocks(HEADS)] * 4
        + [blocks(HEADS), blocks(tiles), blocks(tiles), blocks(HEADS)]
        + [pltpu.VMEM((tiles, TILE, DH), jnp.bfloat16)] * 2
        + [pltpu.VMEM((pairs, TILE, TILE), jnp.bfloat16)] * 2
        + [blocks(HEADS), blocks(tiles), blocks(tiles)]
        + [pltpu.VMEM((pairs, TILE, TILE), jnp.float32)]
        + [
            pltpu.SMEM((tiles, HEADS), jnp.int32),
            pltpu.SemaphoreType.DMA((4,)),
            pltpu.SemaphoreType.DMA((7,)),
            pltpu.SemaphoreType.DMA((5,)),
            pltpu.SemaphoreType.DMA((HEADS,)),
            pltpu.SemaphoreType.DMA((HEADS,)),
        ],
        compiler_params=pltpu.CompilerParams(
            collective_id=0, has_side_effects=True, vmem_limit_bytes=60 * 1024 * 1024
        ),
    )(neighbours.T, counts, queries[0], keys[0], values[0], upstream[0])
    dq, dk, dv = pl.pallas_call(
        functools.partial(unturn, tiles // HEADS),
        out_shape=(out, out, out),
        in_specs=[whole] * 3,
        out_specs=(whole, whole, whole),
        scratch_shapes=[
            blocks(HEADS),
            blocks(tiles),
            blocks(tiles),
            pltpu.VMEM((3, rows, width), jnp.bfloat16),
            pltpu.SemaphoreType.DMA((3,)),
            pltpu.SemaphoreType.DMA((3,)),
        ],
    )(*got)
    return dq[None], dk[None], dv[None]


def solution(mesh):
    spec = P("section", "seq", None)
    return jax.shard_map(
        per_device,
        mesh=mesh,
        in_specs=(spec, spec, spec, spec, P(), P()),
        out_specs=(spec, spec, spec),
        check_vma=False,
    )
```

```python
import functools
import math

import jax
import jax.numpy as jnp
from jax import lax
from jax.experimental import pallas as pl
from jax.experimental.pallas import tpu as pltpu
from jax.sharding import PartitionSpec as P

HEADS = 16
DH = 64
TILE = 128
MAXNB = 6
MASKED = -1e30
MESH = pl.DeviceIdType.MESH
EXPONENT = DH ** (-0.5) * math.log2(math.e)
NT = (((1,), (1,)), ((), ()))


def sweep(step, n, first=0):
    lax.fori_loop(0, n - 1, lambda r, c: step(lax.rem(r + first, n - 1) + 1, c), 0)


def kernel(
    sections,
    tiles,
    near_ref,
    count_ref,
    q_ref,
    k_ref,
    v_ref,
    u_ref,
    dq_got,
    dk_got,
    dv_got,
    q_in,
    k_in,
    v_in,
    u_in,
    q_send,
    k_send,
    v_send,
    u_send,
    q_got,
    k_got,
    v_got,
    u_got,
    k_rows,
    v_rows,
    ds_all,
    pr_all,
    dq_send,
    dk_send,
    dv_send,
    p_all,
    slot_ref,
    load_sem,
    send_sem,
    recv_sem,
    q_sem,
    u_sem,
):
    section = lax.axis_index("section")
    me = lax.axis_index("seq")
    group = me // HEADS
    head = me % HEADS
    behind = lax.rem(section + sections - 1, sections)
    ahead = lax.rem(section + 1, sections)
    pairs = HEADS * MAXNB

    loads = [
        pltpu.make_async_copy(src, dst, load_sem.at[i])
        for i, (src, dst) in enumerate(
            ((k_ref, k_in), (q_ref, q_in), (v_ref, v_in), (u_ref, u_in))
        )
    ]
    for load in loads:
        load.start()
    barrier = pltpu.get_barrier_semaphore()

    def greet(r, c):
        pl.semaphore_signal(
            barrier, inc=1, device_id=(section, lax.rem(me + r, tiles)), device_id_type=MESH
        )
        return c

    def greet_ahead(h, c):
        pl.semaphore_signal(
            barrier, inc=1, device_id=(ahead, group * HEADS + h), device_id_type=MESH
        )
        return c

    lax.fori_loop(1, tiles, greet, 0)
    lax.fori_loop(0, HEADS, greet_ahead, 0)

    def turn(src, dst):
        for c in range(HEADS // 2):
            flipped = src[:, c * 128 : (c + 1) * 128].T
            dst[2 * c] = flipped[:DH]
            dst[2 * c + 1] = flipped[DH:]

    loads[0].wait()
    turn(k_in, k_send)
    loads[1].wait()
    turn(q_in, q_send)
    pl.semaphore_wait(barrier, tiles - 1 + HEADS)

    def remote(src, dst, sent, got, where, peer):
        return pltpu.make_async_remote_copy(
            src_ref=src,
            dst_ref=dst,
            send_sem=sent,
            recv_sem=got,
            device_id=(where, peer),
            device_id_type=MESH,
        )

    def send_keys(buffer, landing, index):
        def step(r, c):
            peer = lax.rem(me + r, tiles)
            remote(
                buffer.at[peer % HEADS],
                landing.at[me],
                send_sem.at[index],
                recv_sem.at[index],
                section,
                peer,
            ).start()
            return c

        sweep(step, tiles)

    def send_queries(buffer, landing, index, sem, where, first, turn_at):
        def step(r, c):
            h = lax.rem(head + r, HEADS)
            remote(
                buffer.at[h],
                landing.at[head],
                send_sem.at[index],
                sem.at[head],
                where,
                group * HEADS + h,
            ).start()
            return c

        if first == 0:
            step(0, 0)
        sweep(step, HEADS, turn_at)

    send_keys(k_send, k_got, 0)
    send_queries(q_send, q_got, 2, q_sem, section, 1, 0)
    loads[2].wait()
    turn(v_in, v_send)
    send_keys(v_send, v_got, 1)
    loads[3].wait()
    turn(u_in, u_send)
    send_queries(u_send, u_got, 3, u_sem, behind, 0, HEADS // 2 - 1)
    k_got[me] = k_send[head]
    v_got[me] = v_send[head]
    q_got[head] = q_send[head]
    ds_all[pairs] = jnp.zeros((TILE, TILE), jnp.bfloat16)
    pr_all[pairs] = jnp.zeros((TILE, TILE), jnp.bfloat16)

    def find(a, c):
        tile = group * HEADS + a
        live = count_ref[tile]
        listed = [
            jnp.where(s < live, near_ref[s, tile], -1) for s in range(MAXNB)
        ]

        def one(b, c):
            found = jnp.int32(pairs)
            for s in range(MAXNB):
                found = jnp.where(listed[s] == b, a * MAXNB + s, found)
            slot_ref[b, a] = found
            return c

        return lax.fori_loop(0, tiles, one, c)

    lax.fori_loop(0, HEADS, find, 0)

    def settle(buffer, count, semaphore):
        part = buffer.at[pl.ds(0, count)]
        pltpu.make_async_copy(part, part, semaphore).wait()

    def upright(src, dst):
        def step(b, c):
            dst[b] = src[b].T
            return c

        lax.fori_loop(0, tiles, step, 0)

    settle(k_got, tiles - 1, recv_sem.at[0])
    upright(k_got, k_rows)

    def weigh(a):
        tile = group * HEADS + a
        live = count_ref[tile]
        query = q_got[a]
        scores = []
        for s in range(MAXNB):
            raw = jnp.dot(
                k_rows[near_ref[s, tile]], query, preferred_element_type=jnp.float32
            )
            scores.append(jnp.where(s < live, raw, MASKED) if s else raw)
        peak = functools.reduce(
            jnp.maximum, [jnp.max(raw, axis=0, keepdims=True) for raw in scores]
        )
        weights = [jnp.exp2((raw - peak) * EXPONENT) for raw in scores]
        share = 1.0 / sum(jnp.sum(w, axis=0, keepdims=True) for w in weights)
        for s in range(MAXNB):
            prob = weights[s] * share
            p_all[a * MAXNB + s] = prob
            pr_all[a * MAXNB + s] = prob.astype(jnp.bfloat16)

    def weigh_step(r, c):
        a = lax.rem(head + HEADS - r, HEADS)
        pltpu.make_async_copy(q_got.at[a], q_got.at[a], q_sem.at[a]).wait()
        weigh(a)
        return c

    weigh(head)
    sweep(weigh_step, HEADS)
    settle(v_got, tiles - 1, recv_sem.at[1])
    upright(v_got, v_rows)

    def query_tile(a):
        tile = group * HEADS + a
        pltpu.make_async_copy(u_got.at[a], u_got.at[a], u_sem.at[a]).wait()
        adjoint = u_got[a]
        near = [near_ref[s, tile] for s in range(MAXNB)]
        probs = [p_all[a * MAXNB + s] for s in range(MAXNB)]
        dprobs = [
            jnp.dot(v_rows[near[s]], adjoint, preferred_element_type=jnp.float32)
            for s in range(MAXNB)
        ]
        delta = sum(
            jnp.sum(p * d, axis=0, keepdims=True) for p, d in zip(probs, dprobs)
        )
        out = jnp.zeros((DH, TILE), jnp.float32)
        for s in range(MAXNB):
            dscore = (probs[s] * (dprobs[s] - delta) * (DH ** (-0.5))).astype(jnp.bfloat16)
            ds_all[a * MAXNB + s] = dscore
            out += jnp.dot(k_got[near[s]], dscore, preferred_element_type=jnp.float32)
        dq_send[a] = out.astype(jnp.bfloat16)

    query_tile(head)

    def query_step(r, c):
        a = lax.rem(head + HEADS - r, HEADS)
        query_tile(a)
        remote(
            dq_send.at[a],
            dq_got.at[head],
            send_sem.at[4],
            recv_sem.at[2],
            section,
            group * HEADS + a,
        ).start()
        return c

    sweep(query_step, HEADS, HEADS // 2 - 1)

    def key_tile(b):
        key_sum = jnp.zeros((DH, TILE), jnp.float32)
        value_sum = jnp.zeros((DH, TILE), jnp.float32)
        for a in range(HEADS):
            slot = slot_ref[b, a]
            key_sum += lax.dot_general(
                q_got[a], ds_all[slot], NT, preferred_element_type=jnp.float32
            )
            value_sum += lax.dot_general(
                u_got[a], pr_all[slot], NT, preferred_element_type=jnp.float32
            )
        dk_send[b] = key_sum.astype(jnp.bfloat16)
        dv_send[b] = value_sum.astype(jnp.bfloat16)

    def key_step(r, c):
        b = lax.rem(me + r, tiles)
        key_tile(b)
        remote(
            dk_send.at[b], dk_got.at[me], send_sem.at[5], recv_sem.at[3], section, b
        ).start()
        remote(
            dv_send.at[b], dv_got.at[me], send_sem.at[6], recv_sem.at[4], section, b
        ).start()
        return c

    sweep(key_step, tiles)
    key_tile(me)
    own = [
        pltpu.make_async_copy(src.at[i], dst.at[i], load_sem.at[n])
        for n, (src, dst, i) in enumerate(
            ((dq_send, dq_got, head), (dk_send, dk_got, me), (dv_send, dv_got, me))
        )
    ]
    for copy in own:
        copy.start()
    for copy in own:
        copy.wait()

    settle(dq_got, HEADS - 1, recv_sem.at[2])
    settle(dk_got, tiles - 1, recv_sem.at[3])
    settle(dv_got, tiles - 1, recv_sem.at[4])
    settle(k_got, tiles - 1, send_sem.at[0])
    settle(v_got, tiles - 1, send_sem.at[1])
    settle(q_got, HEADS - 1, send_sem.at[2])
    settle(u_got, HEADS, send_sem.at[3])
    settle(dq_got, HEADS - 1, send_sem.at[4])
    settle(dk_got, tiles - 1, send_sem.at[5])
    settle(dv_got, tiles - 1, send_sem.at[6])


def unturn(groups, dq_got, dk_got, dv_got, dq_ref, dk_ref, dv_ref, dq, dk, dv, turned, in_sem, out_sem):
    arrays = ((dq_got, dq, dq_ref), (dk_got, dk, dk_ref), (dv_got, dv, dv_ref))
    loads = [
        pltpu.make_async_copy(src, buffer, in_sem.at[n])
        for n, (src, buffer, dst) in enumerate(arrays)
    ]
    for load in loads:
        load.start()
    stores = []
    for n, (src, buffer, dst) in enumerate(arrays):
        loads[n].wait()
        for c in range(HEADS // 2):
            pair = buffer[2 * c : 2 * c + 2]
            if n and groups > 1:
                pair = sum(
                    buffer[g * HEADS + 2 * c : g * HEADS + 2 * c + 2].astype(jnp.float32)
                    for g in range(groups)
                ).astype(jnp.bfloat16)
            turned[n, :, c * 128 : (c + 1) * 128] = pair.reshape(TILE, TILE).T
        stores.append(pltpu.make_async_copy(turned.at[n], dst, out_sem.at[n]))
        stores[n].start()
    for store in stores:
        store.wait()


def per_device(queries, keys, values, upstream, neighbours, counts):
    sections = lax.axis_size("section")
    tiles = lax.axis_size("seq")
    rows, width = queries.shape[1:]
    assert rows == TILE and width == HEADS * DH and tiles % HEADS == 0
    smem = pl.BlockSpec(memory_space=pltpu.SMEM)
    out = jax.ShapeDtypeStruct((rows, width), jnp.bfloat16)

    def blocks(count):
        return pltpu.VMEM((count, DH, TILE), jnp.bfloat16)

    pairs = HEADS * MAXNB + 1
    whole = pl.BlockSpec(memory_space=pl.ANY)

    def shape(count):
        return jax.ShapeDtypeStruct((count, DH, TILE), jnp.bfloat16)

    got = pl.pallas_call(
        functools.partial(kernel, sections, tiles),
        out_shape=(shape(HEADS), shape(tiles), shape(tiles)),
        in_specs=[smem, smem, whole, whole, whole, whole],
        out_specs=(whole,) * 3,
        scratch_shapes=[pltpu.VMEM((rows, width), jnp.bfloat16)] * 4
        + [blocks(HEADS)] * 4
        + [blocks(HEADS), blocks(tiles), blocks(tiles), blocks(HEADS)]
        + [pltpu.VMEM((tiles, TILE, DH), jnp.bfloat16)] * 2
        + [pltpu.VMEM((pairs, TILE, TILE), jnp.bfloat16)] * 2
        + [blocks(HEADS), blocks(tiles), blocks(tiles)]
        + [pltpu.VMEM((pairs, TILE, TILE), jnp.float32)]
        + [
            pltpu.SMEM((tiles, HEADS), jnp.int32),
            pltpu.SemaphoreType.DMA((4,)),
            pltpu.SemaphoreType.DMA((7,)),
            pltpu.SemaphoreType.DMA((5,)),
            pltpu.SemaphoreType.DMA((HEADS,)),
            pltpu.SemaphoreType.DMA((HEADS,)),
        ],
        compiler_params=pltpu.CompilerParams(
            collective_id=0, has_side_effects=True, vmem_limit_bytes=60 * 1024 * 1024
        ),
    )(neighbours.T, counts, queries[0], keys[0], values[0], upstream[0])
    dq, dk, dv = pl.pallas_call(
        functools.partial(unturn, tiles // HEADS),
        out_shape=(out, out, out),
        in_specs=[whole] * 3,
        out_specs=(whole, whole, whole),
        scratch_shapes=[
            blocks(HEADS),
            blocks(tiles),
            blocks(tiles),
            pltpu.VMEM((3, rows, width), jnp.bfloat16),
            pltpu.SemaphoreType.DMA((3,)),
            pltpu.SemaphoreType.DMA((3,)),
        ],
    )(*got)
    return dq[None], dk[None], dv[None]


def solution(mesh):
    spec = P("section", "seq", None)
    return jax.shard_map(
        per_device,
        mesh=mesh,
        in_specs=(spec, spec, spec, spec, P(), P()),
        out_specs=(spec, spec, spec),
        check_vma=False,
    )
```
